32 devices in a mesh: grp: 4 (over z), owner: 8 (over y, x, core).
Axes of the slice: x: 2, y: 2, z: 4, core: 2. Of those that a mesh axis runs over, the one named last changes fastest.
Arguments:
- amplitudes: bfloat16 [256, 2, 64, 3072], P(('grp', 'owner')), may hold values from -6 to 6
- routes: int32 [256, 2], P(('grp', 'owner')), may hold values from 0 to 7, all different within a row; in each aligned block of 8 rows (0 to 7, 8 to 15, ...) at most 2 rows name the same one
- integrals: bfloat16 [24576, 2048], P('owner', 'grp'), may hold values from -0.078125 to 0.078125
Outputs:
- ladder: bfloat16 [256, 64, 2048], P(('grp', 'owner'))
The draws below stay inside these ranges and needn't reach their ends.
Inputs may be any that keep to these rules, and one draw needn't show every extreme that they name: `routes`: each tile row names 2 different panels. Among the tile rows of one device no panel is named more than 2 times, and in every draw some device names some panel exactly 2 times; every panel is named somewhere.
All inputs are finite; a program needn't handle non-finite values.
Results may differ from the reference program's by a relative error of at most 0.0052.
Values may be sent and summed in bfloat16 or wider, within the bound.
A program may use at most 128 MiB of HBM per device.

```python
import math
import jax
import jax.numpy as jnp
import numpy as np
from jax import lax

TILE = 64
CD_OWN = 3072
AB = 2048
K = 2
CAP = 2
ITEMS_DEV = 8
ITEMS = 256
CD = 24576
N_OWNER = 8


def steps_of(own_key, extent, pieces, smallest, top_value):
    factor_of, own = 1.0, jax.random.fold_in(own_key, 6)
    for axis_at, shards_of in pieces:
        heights = jnp.exp(jax.random.uniform(jax.random.fold_in(own, axis_at), (shards_of,), jnp.float32, smallest / len(pieces), top_value / len(pieces)))
        factor_of = factor_of * jnp.repeat(heights, extent[axis_at] // shards_of).reshape([-1 if axis == axis_at else 1 for axis in range(len(extent))])
    return factor_of


def deal_out(rng, own, number, rows, number_of, top, most, skew):
    order = jax.random.permutation(rng, number_of)
    heavy_load, usual = portions_of(number_of, rows * top, most, skew, True), portions_of(number_of, rows * top, most, skew, False)
    places = jnp.arange(number_of)

    def named(sizes, offset_by):
        used = int((sizes > 0).sum())
        fixed = max(1, used // 4)
        passed = fixed + (places - fixed + offset_by * (used - fixed)) % max(1, number_of - fixed)
        return jnp.zeros((number_of,), jnp.int32).at[order[jnp.where(places < fixed, places, passed)]].set(jnp.asarray(sizes, jnp.int32))

    sizes = jnp.where(number % 4 == 0, named(heavy_load, number // 4), named(usual, number - number // 4 - 1))
    mixed = jax.random.permutation(jax.random.fold_in(own, 3), number_of)
    donor, taker = mixed[0:number_of // 2 * 2:2], mixed[1:number_of // 2 * 2:2]
    room = jnp.minimum(sizes[donor] - 1, most - sizes[taker]) // 2
    room = jnp.where((donor == order[0]) | (taker == order[0]) | (sizes[taker] == 0), 0, jnp.maximum(room, 0))
    passed = jax.random.randint(jax.random.fold_in(own, 4), (number_of // 2,), 0, 1 << 20) % (room + 1)
    sizes = sizes.at[donor].add(-passed).at[taker].add(passed)
    labels = jnp.searchsorted(jnp.cumsum(sizes), jnp.arange(rows * top), side="right").astype(jnp.int32)
    grid = labels.reshape(top, rows).T
    grid = grid[jax.random.permutation(jax.random.fold_in(own, 1), rows)]
    offset_by = jax.random.randint(jax.random.fold_in(own, 2), (rows, 1), 0, top)
    return jnp.take_along_axis(grid, (jnp.arange(top)[None, :] + offset_by) % top, axis=1)


def portions_of(amount, total, reach, slope, full):
    weights = [(1 << 20) // math.isqrt(grade ** slope) + 1 for grade in range(1, amount + 1)]
    largest = reach if full else min(reach, max(-(-total // amount), total * weights[0] // sum(weights)))
    least = 1 if total - largest >= amount - 1 else 0
    holding, spare = [largest] + [least] * (amount - 1), total - largest - least * (amount - 1)
    while spare > 0:
        candidates = [i for i in range(1, amount) if holding[i] < largest] or [i for i in range(1, amount) if holding[i] < reach]
        mass, remaining = sum([weights[i] for i in candidates]), spare
        for i in candidates:
            extra = min(reach - holding[i], max(1, remaining * weights[i] // mass), spare)
            holding[i] = holding[i] + extra
            spare = spare - extra
    return np.array(holding)


def scatter_about(rng, dims, deviation, bound, cuts=(), held_as=jnp.bfloat16):
    drawn = jax.random.normal(rng, dims, jnp.float32) * deviation
    if len(cuts) > 0:
        drawn = steps_of(rng, dims, cuts, -0.22, 0.18) * drawn
    return jnp.clip(drawn, min=-bound, max=bound).astype(held_as)


def setup_inputs(seed: int = 0) -> dict:
    seeds = jax.random.split(jax.random.key(seed), 4)
    amplitudes = scatter_about(seeds[0], (ITEMS, K, TILE, CD_OWN), 1.0, 6.0, ((0, 32),))
    routes_keys = jax.random.split(jax.random.fold_in(seeds[1], 1), ITEMS // ITEMS_DEV)
    routes_turns = jax.random.permutation(jax.random.fold_in(seeds[1], 3), ITEMS // ITEMS_DEV)
    routes = jax.vmap(lambda own, number: deal_out(jax.random.fold_in(seeds[1], 2), own, number, ITEMS_DEV, N_OWNER, K, CAP, 2))(routes_keys, routes_turns).reshape((ITEMS, K))
    integrals = scatter_about(seeds[2], (CD, AB), (K * CD_OWN) ** -0.5, 0.078125, ((0, 8), (1, 4)))
    return dict(amplitudes=amplitudes, routes=routes, integrals=integrals)


def reference(amplitudes, routes, integrals):
    panels = integrals.reshape(N_OWNER, CD_OWN, AB).astype(jnp.float32)

    def one_row(pair_args):
        row_blocks, owner_ids = pair_args
        running = jnp.zeros((TILE, AB), jnp.float32)
        for which in range(K):
            product = jnp.dot(row_blocks[which].astype(jnp.float32), panels[owner_ids[which]], precision=lax.Precision.HIGHEST)
            rounded = lax.optimization_barrier(product.astype(jnp.bfloat16))
            running = running + rounded.astype(jnp.float32)
        return running.astype(jnp.bfloat16)

    return lax.map(one_row, (amplitudes, routes))
```

```python
import functools

import jax
import jax.numpy as jnp
from jax import lax
from jax.experimental import pallas as pl
from jax.experimental.pallas import tpu as pltpu
from jax.sharding import PartitionSpec as P

CAP = 2
HALVES = 2
PARTS = 4
CHUNKS = HALVES * PARTS
MESH = pl.DeviceIdType.MESH


def local(amplitudes, routes, integrals):
    tile_rows, per_row, tile_edge, panel_rows = amplitudes.shape
    owner_count = lax.axis_size("owner")
    capacity = CAP
    entries = tile_rows * per_row
    flat_dest = routes.reshape(entries)
    onehot = (flat_dest[:, None] == jnp.arange(owner_count, dtype=jnp.int32)[None, :]).astype(
        jnp.int32
    )
    slot_rank = jnp.sum((jnp.cumsum(onehot, axis=0) - onehot) * onehot, axis=1)
    slot_index = flat_dest * capacity + slot_rank
    slot_total = owner_count * capacity
    matches = slot_index[None, :] == jnp.arange(slot_total, dtype=jnp.int32)[:, None]
    filled = jnp.any(matches, axis=1)
    source_entry = jnp.sum(
        matches.astype(jnp.int32) * jnp.arange(entries, dtype=jnp.int32)[None, :], axis=1
    )
    amp_blocks = amplitudes.reshape(entries, tile_edge, panel_rows)
    outgoing = jnp.where(
        filled[:, None, None],
        jnp.take(amp_blocks, source_entry, axis=0),
        jnp.zeros((), amplitudes.dtype),
    )
    outgoing = outgoing.reshape(owner_count, capacity, tile_edge, panel_rows)
    incoming = lax.all_to_all(outgoing, "owner", split_axis=0, concat_axis=0, tiled=True)
    stacked = incoming.reshape(-1, panel_rows)
    computed = jnp.dot(
        stacked,
        lax.all_gather(integrals, "grp", axis=1, tiled=True),
        preferred_element_type=jnp.float32,
    ).astype(jnp.bfloat16)
    computed = computed.reshape(owner_count, capacity, tile_edge, computed.shape[-1])
    returned = lax.all_to_all(computed, "owner", split_axis=0, concat_axis=0, tiled=True)
    out_width = returned.shape[-1]
    picked = jnp.take(returned.reshape(slot_total, tile_edge, out_width), slot_index, axis=0)
    picked = picked.reshape(tile_rows, per_row, tile_edge, out_width).astype(jnp.float32)
    return jnp.sum(picked, axis=1).astype(jnp.bfloat16)


def kernel(
    n_o, dims, routes, amp_hbm, int_hbm, out, amp, stage, inc, panels, prod, ret, table,
    amp_send, amp_recv, sh_send, sh_recv, ret_send, ret_recv, load_sem, own_sem, self_sem,
):
    rows, k_of, edge_len, depth, width = dims
    entries = rows * k_of
    half, part = width // HALVES, depth // PARTS
    g, me = lax.axis_index("grp"), lax.axis_index("owner")
    is_edge = (g == 0) | (g == 3)
    is_mid = (g == 1) | (g == 2)
    odd = me % 2
    pair = g + 1 - 2 * (g % 2)
    inner, far = 3 - g, 3 - pair

    amp_load = pltpu.make_async_copy(amp_hbm, amp, load_sem)
    amp_load.start()

    def own_load(h):
        return pltpu.make_async_copy(
            int_hbm.at[:, pl.ds(h * half, half)], panels.at[g, h], own_sem.at[h]
        )

    for h in range(HALVES):
        own_load(h).start()

    barrier = pltpu.get_barrier_semaphore()

    @pl.loop(0, n_o)
    def _(o):
        @pl.when(o != me)
        def _():
            pl.semaphore_signal(barrier, inc=1, device_id=(g, o), device_id_type=MESH)

        pl.semaphore_signal(barrier, inc=1, device_id=(pair, o), device_id_type=MESH)

    @pl.when(is_mid)
    def _():
        pl.semaphore_signal(barrier, inc=1, device_id=(inner, me), device_id_type=MESH)
        pl.semaphore_wait(barrier, 2 * n_o)

    @pl.when(is_edge)
    def _():
        pl.semaphore_wait(barrier, 2 * n_o - 1)

    def own_shard(c, lane, to):
        h, q = c // PARTS, c % PARTS
        return pltpu.make_async_remote_copy(
            src_ref=int_hbm.at[pl.ds(q * part, part), pl.ds(h * half, half)],
            dst_ref=panels.at[g, h, pl.ds(q * part, part)],
            send_sem=sh_send.at[lane, c],
            recv_sem=sh_recv.at[g, c],
            device_id=(to, me),
            device_id_type=MESH,
        )

    def shard(s, c, lane, to):
        h, q = c // PARTS, c % PARTS
        piece = panels.at[s, h, pl.ds(q * part, part)]
        return pltpu.make_async_remote_copy(
            src_ref=piece,
            dst_ref=piece,
            send_sem=sh_send.at[lane, c],
            recv_sem=sh_recv.at[s, c],
            device_id=(to, me),
            device_id_type=MESH,
        )

    @pl.when(is_mid)
    def _():
        for c in range(CHUNKS):
            own_shard(c, 0, inner).start()

            @pl.when(odd == 1)
            def _():
                own_shard(c, 1, pair).start()

    dest = [routes[e // k_of, e % k_of] for e in range(entries)]
    rank = []
    for e in range(entries):
        total = jnp.int32(0)
        for b in range(e):
            total += (dest[b] == dest[e]).astype(jnp.int32)
        rank.append(jnp.minimum(total, CAP - 1))
    for slot in range(n_o * CAP):
        total = jnp.int32(0)
        for e in range(entries):
            total += jnp.where(dest[e] * CAP + rank[e] == slot, e, 0)
        table[slot] = jnp.minimum(total, entries - 1)

    def amp_copy(o, to, which):
        return pltpu.make_async_remote_copy(
            src_ref=stage.at[o],
            dst_ref=inc.at[which, me],
            send_sem=amp_send.at[o],
            recv_sem=amp_recv.at[which, me],
            device_id=(to, o),
            device_id_type=MESH,
        )

    def amp_self():
        return pltpu.make_async_copy(stage.at[me], inc.at[0, me], amp_recv.at[0, me])

    amp_load.wait()

    @pl.loop(0, n_o)
    def _(t):
        second = t // (n_o // 2)
        o = 2 * ((me // 2 + t) % (n_o // 2)) + second
        for c in range(CAP):
            stage[o, c] = amp[table[o * CAP + c]]
        away = is_edge & (second == 0)

        @pl.when(away)
        def _():
            amp_copy(o, pair, 1).start()

        @pl.when(jnp.logical_not(away) & (o != me))
        def _():
            amp_copy(o, g, 0).start()

        @pl.when(jnp.logical_not(away) & (o == me))
        def _():
            amp_self().start()

    @pl.when(is_edge)
    def _():
        @pl.loop(0, n_o // 2)
        def _(i):
            amp_copy(2 * i, pair, 1).wait_send()

        for c in range(CHUNKS):
            own_shard(c, 0, pair).start()

    for h in range(HALVES):
        own_load(h).wait()

    def wait_amps(which):
        @pl.loop(0, n_o)
        def _(j):
            @pl.when((j != me) | (which == 1))
            def _():
                pltpu.make_async_remote_copy(
                    src_ref=stage.at[j],
                    dst_ref=inc.at[which, j],
                    send_sem=amp_send.at[j],
                    recv_sem=amp_recv.at[which, j],
                    device_id=(pair, j),
                    device_id_type=MESH,
                ).wait_recv()

            @pl.when((j == me) & (which == 0))
            def _():
                amp_self().wait()

    def ret_copy(which, s, h, j):
        return pltpu.make_async_remote_copy(
            src_ref=prod.at[which, s, h, j],
            dst_ref=ret.at[s, h, me],
            send_sem=ret_send.at[which, s, h, j],
            recv_sem=ret_recv.at[s, h, me],
            device_id=(jnp.where(which == 1, pair, g), j),
            device_id_type=MESH,
        )

    def ret_self(s, h):
        return pltpu.make_async_copy(prod.at[0, s, h, me], ret.at[s, h, me], self_sem.at[s, h])

    group = max(1, n_o // 2)

    def compute(which, s, h):
        @pl.loop(0, n_o // group)
        def _(b):
            lhs = inc[which, pl.ds(b * group, group)].reshape(group * CAP * edge_len, depth)
            got = jnp.dot(lhs, panels[s, h], preferred_element_type=jnp.float32)
            prod[which, s, h, pl.ds(b * group, group)] = got.astype(jnp.bfloat16).reshape(
                group, CAP, edge_len, half
            )

            @pl.loop(0, group)
            def _(i):
                j = b * group + i
                remote = (j != me) | (which == 1)

                @pl.when(remote)
                def _():
                    ret_copy(which, s, h, j).start()

                @pl.when(jnp.logical_not(remote))
                def _():
                    ret_self(s, h).start()

    @pl.when(is_mid)
    def _():
        @pl.loop(0, CHUNKS)
        def _(c):
            shard(inner, c, 2, pair).wait_recv()

            @pl.when(odd == 1)
            def _():
                shard(inner, c, 2, pair).start()

        wait_amps(0)

        @pl.loop(0, 2)
        def _(h):
            compute(0, g, h)

        @pl.loop(0, CHUNKS)
        def _(c):
            shard(pair, c, 4, inner).wait_recv()
            shard(pair, c, 4, inner).start()
            shard(far, c, 3, pair).wait_recv()

            @pl.when(odd == 1)
            def _():
                shard(far, c, 3, pair).start()

            @pl.when(c < 2)
            def _():
                compute(0, inner, c)

            @pl.when((c == 2) & (odd == 0))
            def _():
                wait_amps(1)

            @pl.when((c >= 2) & (c < 4) & (odd == 0))
            def _():
                @pl.loop(0, 2)
                def _(h):
                    compute(1, jnp.where(c == 2, g, inner), h)

            @pl.when((c >= 4) & ((c < 6) | (odd == 0)))
            def _():
                compute(c // 6, jnp.where(c % 2 == 0, pair, far), 0)

        @pl.loop(0, 4)
        def _(i):
            @pl.when((i >= 2) | (odd == 0))
            def _():
                compute(1 - i // 2, jnp.where(i % 2 == 0, pair, far), 1)

    @pl.when(is_edge & (odd == 1))
    def _():
        wait_amps(0)

        @pl.loop(0, 4 * HALVES)
        def _(i):
            step, h = i // HALVES, i % HALVES
            s = jnp.where(step == 0, g, jnp.where(step == 1, pair, jnp.where(step == 2, 3 - pair, 3 - g)))

            @pl.when(step > 0)
            def _():
                @pl.loop(0, PARTS)
                def _(q):
                    shard(s, h * PARTS + q, 0, pair).wait_recv()

            compute(0, s, h)

    @pl.loop(0, 4 * HALVES)
    def _(i):
        s, h = i // HALVES, i % HALVES

        @pl.loop(0, n_o)
        def _(o):
            mine = (o == me) & (is_mid | (odd == 1))

            @pl.when(jnp.logical_not(mine))
            def _():
                pltpu.make_async_remote_copy(
                    src_ref=prod.at[0, s, h, o],
                    dst_ref=ret.at[s, h, o],
                    send_sem=ret_send.at[0, s, h, o],
                    recv_sem=ret_recv.at[s, h, o],
                    device_id=(pair, o),
                    device_id_type=MESH,
                ).wait_recv()

            @pl.when(mine)
            def _():
                ret_self(s, h).wait()

    for i in range(rows):
        for s in range(4):
            for h in range(HALVES):
                total = jnp.zeros((edge_len, half), jnp.float32)
                for k in range(k_of):
                    e = i * k_of + k
                    total += ret[s, h, dest[e], rank[e]].astype(jnp.float32)
                out[i, :, s * width + h * half : s * width + (h + 1) * half] = total.astype(
                    jnp.bfloat16
                )

    @pl.loop(0, n_o)
    def _(o):
        @pl.when(is_mid & (o != me))
        def _():
            amp_copy(o, g, 0).wait_send()

        @pl.when(is_edge & (o % 2 == 1) & (o != me))
        def _():
            amp_copy(o, g, 0).wait_send()

    @pl.loop(0, CHUNKS)
    def _(c):
        own_shard(c, 0, pair).wait_send()

        @pl.when(is_mid)
        def _():
            shard(pair, c, 4, inner).wait_send()

        @pl.when(is_mid & (odd == 1))
        def _():
            own_shard(c, 1, pair).wait_send()
            shard(inner, c, 2, pair).wait_send()
            shard(far, c, 3, pair).wait_send()

    @pl.loop(0, 4 * HALVES)
    def _(i):
        s, h = i // HALVES, i % HALVES

        @pl.loop(0, n_o)
        def _(j):
            @pl.when((j != me) & (is_mid | (odd == 1)))
            def _():
                ret_copy(0, s, h, j).wait_send()

            @pl.when(is_mid & (odd == 0))
            def _():
                ret_copy(1, s, h, j).wait_send()


def fused(amplitudes, routes, integrals):
    rows, k_of, edge_len, depth = amplitudes.shape
    width = integrals.shape[1]
    n_o, n_g = lax.axis_size("owner"), lax.axis_size("grp")
    half = width // HALVES
    amps = amplitudes.reshape(rows * k_of, edge_len, depth)
    block = (CAP, edge_len)
    dma = pltpu.SemaphoreType.DMA
    return pl.pallas_call(
        functools.partial(kernel, n_o, (rows, k_of, edge_len, depth, width)),
        out_shape=jax.ShapeDtypeStruct((rows, edge_len, n_g * width), jnp.bfloat16),
        in_specs=[
            pl.BlockSpec(memory_space=pltpu.SMEM),
            pl.BlockSpec(memory_space=pl.ANY),
            pl.BlockSpec(memory_space=pl.ANY),
        ],
        out_specs=pl.BlockSpec(memory_space=pltpu.VMEM),
        scratch_shapes=[
            pltpu.VMEM(amps.shape, jnp.bfloat16),
            pltpu.VMEM((n_o, *block, depth), jnp.bfloat16),
            pltpu.VMEM((2, n_o, *block, depth), jnp.bfloat16),
            pltpu.VMEM((n_g, HALVES, depth, half), jnp.bfloat16),
            pltpu.VMEM((2, n_g, HALVES, n_o, *block, half), jnp.bfloat16),
            pltpu.VMEM((n_g, HALVES, n_o, *block, half), jnp.bfloat16),
            pltpu.SMEM((n_o * CAP,), jnp.int32),
            dma((n_o,)),
            dma((2, n_o)),
            dma((5, CHUNKS)),
            dma((n_g, CHUNKS)),
            dma((2, n_g, HALVES, n_o)),
            dma((n_g, HALVES, n_o)),
            dma,
            dma((HALVES,)),
            dma((n_g, HALVES)),
        ],
        compiler_params=pltpu.CompilerParams(
            collective_id=0, has_side_effects=True, vmem_limit_bytes=60 << 20
        ),
        name="ladder",
    )(routes, amps, integrals)


def solution(mesh):
    in_specs = (P(("grp", "owner"), None, None, None), P(("grp", "owner"), None), P("owner", "grp"))
    out_specs = P(("grp", "owner"), None, None)
    body = fused if mesh.shape["grp"] == 4 and mesh.shape["owner"] % 2 == 0 else local
    return jax.shard_map(body, mesh=mesh, in_specs=in_specs, out_specs=out_specs, check_vma=False)
```

```python
import functools

import jax
import jax.numpy as jnp
from jax import lax
from jax.experimental import pallas as pl
from jax.experimental.pallas import tpu as pltpu
from jax.sharding import PartitionSpec as P

CAP = 2
HALVES = 2
PARTS = 4
CHUNKS = HALVES * PARTS
MESH = pl.DeviceIdType.MESH


def local(amplitudes, routes, integrals):
    tile_rows, per_row, tile_edge, panel_rows = amplitudes.shape
    owner_count = lax.axis_size("owner")
    capacity = CAP
    entries = tile_rows * per_row
    flat_dest = routes.reshape(entries)
    onehot = (flat_dest[:, None] == jnp.arange(owner_count, dtype=jnp.int32)[None, :]).astype(
        jnp.int32
    )
    slot_rank = jnp.sum((jnp.cumsum(onehot, axis=0) - onehot) * onehot, axis=1)
    slot_index = flat_dest * capacity + slot_rank
    slot_total = owner_count * capacity
    matches = slot_index[None, :] == jnp.arange(slot_total, dtype=jnp.int32)[:, None]
    filled = jnp.any(matches, axis=1)
    source_entry = jnp.sum(
        matches.astype(jnp.int32) * jnp.arange(entries, dtype=jnp.int32)[None, :], axis=1
    )
    amp_blocks = amplitudes.reshape(entries, tile_edge, panel_rows)
    outgoing = jnp.where(
        filled[:, None, None],
        jnp.take(amp_blocks, source_entry, axis=0),
        jnp.zeros((), amplitudes.dtype),
    )
    outgoing = outgoing.reshape(owner_count, capacity, tile_edge, panel_rows)
    incoming = lax.all_to_all(outgoing, "owner", split_axis=0, concat_axis=0, tiled=True)
    stacked = incoming.reshape(-1, panel_rows)
    computed = jnp.dot(
        stacked,
        lax.all_gather(integrals, "grp", axis=1, tiled=True),
        preferred_element_type=jnp.float32,
    ).astype(jnp.bfloat16)
    computed = computed.reshape(owner_count, capacity, tile_edge, computed.shape[-1])
    returned = lax.all_to_all(computed, "owner", split_axis=0, concat_axis=0, tiled=True)
    out_width = returned.shape[-1]
    picked = jnp.take(returned.reshape(slot_total, tile_edge, out_width), slot_index, axis=0)
    picked = picked.reshape(tile_rows, per_row, tile_edge, out_width).astype(jnp.float32)
    return jnp.sum(picked, axis=1).astype(jnp.bfloat16)


def kernel(
    n_o, dims, routes, amp_hbm, int_hbm, out, amp, stage, inc, panels, prod, ret, table,
    amp_send, amp_recv, relay_send, sh_send, sh_recv, ret_send, ret_recv, load_sem, own_sem, self_sem,
):
    rows, k_of, edge_len, depth, width = dims
    entries = rows * k_of
    half, part = width // HALVES, depth // PARTS
    g, me = lax.axis_index("grp"), lax.axis_index("owner")
    is_edge = (g == 0) | (g == 3)
    is_mid = (g == 1) | (g == 2)
    odd = me % 2
    pair = g + 1 - 2 * (g % 2)
    inner, far = 3 - g, 3 - pair

    amp_load = pltpu.make_async_copy(amp_hbm, amp, load_sem)
    amp_load.start()

    def own_load(h):
        return pltpu.make_async_copy(
            int_hbm.at[:, pl.ds(h * half, half)], panels.at[g, h], own_sem.at[h]
        )

    for h in range(HALVES):
        own_load(h).start()

    barrier = pltpu.get_barrier_semaphore()

    @pl.loop(0, n_o)
    def _(o):
        @pl.when(o != me)
        def _():
            pl.semaphore_signal(barrier, inc=1, device_id=(g, o), device_id_type=MESH)

        pl.semaphore_signal(barrier, inc=1, device_id=(pair, o), device_id_type=MESH)

    @pl.when(is_mid)
    def _():
        pl.semaphore_signal(barrier, inc=1, device_id=(inner, me), device_id_type=MESH)
        pl.semaphore_wait(barrier, 2 * n_o)

    @pl.when(is_edge)
    def _():
        pl.semaphore_wait(barrier, 2 * n_o - 1)

    def own_shard(c, lane, to):
        h, q = c // PARTS, c % PARTS
        return pltpu.make_async_remote_copy(
            src_ref=int_hbm.at[pl.ds(q * part, part), pl.ds(h * half, half)],
            dst_ref=panels.at[g, h, pl.ds(q * part, part)],
            send_sem=sh_send.at[lane, c],
            recv_sem=sh_recv.at[g, c],
            device_id=(to, me),
            device_id_type=MESH,
        )

    def shard(s, c, lane, to):
        h, q = c // PARTS, c % PARTS
        piece = panels.at[s, h, pl.ds(q * part, part)]
        return pltpu.make_async_remote_copy(
            src_ref=piece,
            dst_ref=piece,
            send_sem=sh_send.at[lane, c],
            recv_sem=sh_recv.at[s, c],
            device_id=(to, me),
            device_id_type=MESH,
        )

    @pl.when(is_edge & (odd == 1))
    def _():
        for c in range(CHUNKS):
            own_shard(c, 0, pair).start()

    @pl.when(is_mid)
    def _():
        for c in range(CHUNKS):
            own_shard(c, 0, inner).start()

            @pl.when(odd == 1)
            def _():
                own_shard(c, 1, pair).start()

    dest = [routes[e // k_of, e % k_of] for e in range(entries)]
    rank = []
    for e in range(entries):
        total = jnp.int32(0)
        for b in range(e):
            total += (dest[b] == dest[e]).astype(jnp.int32)
        rank.append(jnp.minimum(total, CAP - 1))
    for slot in range(n_o * CAP):
        total = jnp.int32(0)
        for e in range(entries):
            total += jnp.where(dest[e] * CAP + rank[e] == slot, e, 0)
        table[slot] = jnp.minimum(total, entries - 1)

    def amp_copy(o, to, which):
        return pltpu.make_async_remote_copy(
            src_ref=stage.at[o],
            dst_ref=inc.at[which, me],
            send_sem=amp_send.at[o],
            recv_sem=amp_recv.at[which, me],
            device_id=(to, o),
            device_id_type=MESH,
        )

    def amp_self():
        return pltpu.make_async_copy(stage.at[me], inc.at[0, me], amp_recv.at[0, me])

    amp_load.wait()

    @pl.loop(0, n_o)
    def _(t):
        second = t // (n_o // 2)
        o = 2 * ((me // 2 + t) % (n_o // 2)) + second
        for c in range(CAP):
            stage[o, c] = amp[table[o * CAP + c]]

        @pl.when(o != me)
        def _():
            amp_copy(o, g, 0).start()

        @pl.when(o == me)
        def _():
            amp_self().start()

    for h in range(HALVES):
        own_load(h).wait()

    def wait_amps(which):
        @pl.loop(0, n_o)
        def _(j):
            @pl.when((j != me) | (which == 1))
            def _():
                pltpu.make_async_remote_copy(
                    src_ref=stage.at[j],
                    dst_ref=inc.at[which, j],
                    send_sem=amp_send.at[j],
                    recv_sem=amp_recv.at[which, j],
                    device_id=(pair, j),
                    device_id_type=MESH,
                ).wait_recv()

            @pl.when((j == me) & (which == 0))
            def _():
                amp_self().wait()

    def relay(j):
        return pltpu.make_async_remote_copy(
            src_ref=inc.at[0, j],
            dst_ref=inc.at[1, j],
            send_sem=relay_send.at[j],
            recv_sem=amp_recv.at[1, j],
            device_id=(pair, me),
            device_id_type=MESH,
        )

    @pl.when(is_edge & (odd == 0))
    def _():
        amp_self().wait()
        relay(me).start()

        @pl.loop(1, n_o)
        def _(t):
            j = (me + n_o - t) % n_o
            pltpu.make_async_remote_copy(
                src_ref=stage.at[j],
                dst_ref=inc.at[0, j],
                send_sem=amp_send.at[j],
                recv_sem=amp_recv.at[0, j],
                device_id=(g, j),
                device_id_type=MESH,
            ).wait_recv()
            relay(j).start()

        for c in range(CHUNKS):
            own_shard(c, 0, pair).start()

    def ret_copy(which, s, h, j):
        return pltpu.make_async_remote_copy(
            src_ref=prod.at[which, s, h, j],
            dst_ref=ret.at[s, h, me],
            send_sem=ret_send.at[which, s, h, j],
            recv_sem=ret_recv.at[s, h, me],
            device_id=(jnp.where(which == 1, pair, g), j),
            device_id_type=MESH,
        )

    def ret_self(s, h):
        return pltpu.make_async_copy(prod.at[0, s, h, me], ret.at[s, h, me], self_sem.at[s, h])

    group = max(1, n_o // 2)

    def compute(which, s, h):
        @pl.loop(0, n_o // group)
        def _(b):
            lhs = inc[which, pl.ds(b * group, group)].reshape(group * CAP * edge_len, depth)
            got = jnp.dot(lhs, panels[s, h], preferred_element_type=jnp.float32)
            prod[which, s, h, pl.ds(b * group, group)] = got.astype(jnp.bfloat16).reshape(
                group, CAP, edge_len, half
            )

            @pl.loop(0, group)
            def _(i):
                j = b * group + i
                remote = (j != me) | (which == 1)

                @pl.when(remote)
                def _():
                    ret_copy(which, s, h, j).start()

                @pl.when(jnp.logical_not(remote))
                def _():
                    ret_self(s, h).start()

    @pl.when(is_mid)
    def _():
        @pl.loop(0, CHUNKS)
        def _(c):
            shard(inner, c, 2, pair).wait_recv()

            @pl.when(odd == 1)
            def _():
                shard(inner, c, 2, pair).start()
                shard(pair, c, 4, inner).wait_recv()
                shard(pair, c, 4, inner).start()

        wait_amps(0)

        @pl.loop(0, 2)
        def _(h):
            compute(0, g, h)

        @pl.loop(0, CHUNKS)
        def _(c):
            @pl.when(odd == 0)
            def _():
                shard(pair, c, 4, inner).wait_recv()
                shard(pair, c, 4, inner).start()

            shard(far, c, 3, pair).wait_recv()

            @pl.when(odd == 1)
            def _():
                shard(far, c, 3, pair).start()

            @pl.when(c < 2)
            def _():
                compute(0, inner, c)

            @pl.when((c == 2) & (odd == 0))
            def _():
                wait_amps(1)

            @pl.when((c >= 2) & (c < 4) & (odd == 0))
            def _():
                @pl.loop(0, 2)
                def _(h):
                    compute(1, jnp.where(c == 2, g, inner), h)

            @pl.when((c >= 4) & ((c < 6) | (odd == 0)))
            def _():
                compute(c // 6, jnp.where(c % 2 == 0, pair, far), 0)

        @pl.loop(0, 4)
        def _(i):
            @pl.when((i >= 2) | (odd == 0))
            def _():
                compute(1 - i // 2, jnp.where(i % 2 == 0, pair, far), 1)

    @pl.when(is_edge & (odd == 1))
    def _():
        wait_amps(0)

        @pl.loop(0, 4 * HALVES)
        def _(i):
            step, h = i // HALVES, i % HALVES
            s = jnp.where(step == 0, g, jnp.where(step == 1, pair, jnp.where(step == 2, 3 - pair, 3 - g)))

            @pl.when(step > 0)
            def _():
                @pl.loop(0, PARTS)
                def _(q):
                    shard(s, h * PARTS + q, 0, pair).wait_recv()

            compute(0, s, h)

    @pl.loop(0, 4 * HALVES)
    def _(i):
        s, h = i // HALVES, i % HALVES

        @pl.loop(0, n_o)
        def _(o):
            mine = (o == me) & (is_mid | (odd == 1))

            @pl.when(jnp.logical_not(mine))
            def _():
                pltpu.make_async_remote_copy(
                    src_ref=prod.at[0, s, h, o],
                    dst_ref=ret.at[s, h, o],
                    send_sem=ret_send.at[0, s, h, o],
                    recv_sem=ret_recv.at[s, h, o],
                    device_id=(pair, o),
                    device_id_type=MESH,
                ).wait_recv()

            @pl.when(mine)
            def _():
                ret_self(s, h).wait()

    for i in range(rows):
        for s in range(4):
            for h in range(HALVES):
                total = jnp.zeros((edge_len, half), jnp.float32)
                for k in range(k_of):
                    e = i * k_of + k
                    total += ret[s, h, dest[e], rank[e]].astype(jnp.float32)
                out[i, :, s * width + h * half : s * width + (h + 1) * half] = total.astype(
                    jnp.bfloat16
                )

    @pl.loop(0, n_o)
    def _(o):
        @pl.when(o != me)
        def _():
            amp_copy(o, g, 0).wait_send()

        @pl.when(is_edge & (odd == 0))
        def _():
            relay(o).wait_send()

    @pl.loop(0, CHUNKS)
    def _(c):
        own_shard(c, 0, pair).wait_send()

        @pl.when(is_mid)
        def _():
            shard(pair, c, 4, inner).wait_send()

        @pl.when(is_mid & (odd == 1))
        def _():
            own_shard(c, 1, pair).wait_send()
            shard(inner, c, 2, pair).wait_send()
            shard(far, c, 3, pair).wait_send()

    @pl.loop(0, 4 * HALVES)
    def _(i):
        s, h = i // HALVES, i % HALVES

        @pl.loop(0, n_o)
        def _(j):
            @pl.when((j != me) & (is_mid | (odd == 1)))
            def _():
                ret_copy(0, s, h, j).wait_send()

            @pl.when(is_mid & (odd == 0))
            def _():
                ret_copy(1, s, h, j).wait_send()


def fused(amplitudes, routes, integrals):
    rows, k_of, edge_len, depth = amplitudes.shape
    width = integrals.shape[1]
    n_o, n_g = lax.axis_size("owner"), lax.axis_size("grp")
    half = width // HALVES
    amps = amplitudes.reshape(rows * k_of, edge_len, depth)
    block = (CAP, edge_len)
    dma = pltpu.SemaphoreType.DMA
    return pl.pallas_call(
        functools.partial(kernel, n_o, (rows, k_of, edge_len, depth, width)),
        out_shape=jax.ShapeDtypeStruct((rows, edge_len, n_g * width), jnp.bfloat16),
        in_specs=[
            pl.BlockSpec(memory_space=pltpu.SMEM),
            pl.BlockSpec(memory_space=pl.ANY),
            pl.BlockSpec(memory_space=pl.ANY),
        ],
        out_specs=pl.BlockSpec(memory_space=pltpu.VMEM),
        scratch_shapes=[
            pltpu.VMEM(amps.shape, jnp.bfloat16),
            pltpu.VMEM((n_o, *block, depth), jnp.bfloat16),
            pltpu.VMEM((2, n_o, *block, depth), jnp.bfloat16),
            pltpu.VMEM((n_g, HALVES, depth, half), jnp.bfloat16),
            pltpu.VMEM((2, n_g, HALVES, n_o, *block, half), jnp.bfloat16),
            pltpu.VMEM((n_g, HALVES, n_o, *block, half), jnp.bfloat16),
            pltpu.SMEM((n_o * CAP,), jnp.int32),
            dma((n_o,)),
            dma((2, n_o)),
            dma((n_o,)),
            dma((5, CHUNKS)),
            dma((n_g, CHUNKS)),
            dma((2, n_g, HALVES, n_o)),
            dma((n_g, HALVES, n_o)),
            dma,
            dma((HALVES,)),
            dma((n_g, HALVES)),
        ],
        compiler_params=pltpu.CompilerParams(
            collective_id=0, has_side_effects=True, vmem_limit_bytes=60 << 20
        ),
        name="ladder",
    )(routes, amps, integrals)


def solution(mesh):
    in_specs = (P(("grp", "owner"), None, None, None), P(("grp", "owner"), None), P("owner", "grp"))
    out_specs = P(("grp", "owner"), None, None)
    body = fused if mesh.shape["grp"] == 4 and mesh.shape["owner"] % 2 == 0 else local
    return jax.shard_map(body, mesh=mesh, in_specs=in_specs, out_specs=out_specs, check_vma=False)
```
